128 devices in a mesh: gx: 4 (over y), gy: 32 (over z, x, core).
Axes of the slice: x: 4, y: 4, z: 4, core: 2. Of those that a mesh axis runs over, the one named last changes fastest.
Arguments:
- labels: float32 [524288, 256], P(('gx', 'gy')), may hold values from 0 to 24, as said below
- weights: bfloat16 [4096, 12, 128, 128], P(('gx', 'gy')), may hold values from 0.001 to 1, as said below
- column_index: int32 [4096, 12], P(('gx', 'gy')), may hold values from 0 to 47, as said below
- send_index: int32 [128, 4, 4], P(('gx', 'gy')), may hold values from 0 to 31, as said below
- seed_doc: int32 [32768], P(('gx', 'gy')), may hold values from 0 to 4095
- seed_topic: int32 [32768], P(('gx', 'gy')), may hold values from 0 to 255
Outputs:
- spread: float32 [524288, 256], P(('gx', 'gy'))
The draws below stay inside these ranges and needn't reach their ends.
Inputs may be any that keep to these rules, and one draw needn't show every extreme that they name: `column_index`: slot 0 of a row block names the row block itself (its index within the partition). A value below 32 names a block of the partition's own labels; 32 + d * 4 + s names slot s of what neighbour d hands over; only existing neighbours are named, and only in the last 3 slots. `send_index`: the 4 entries of one partition and direction are distinct. `weights`: entries are positive. `labels`: entries are nonnegative.
All inputs are finite; a program needn't handle non-finite values.
Results may differ from the reference program's by a relative error of at most 0.0004.
Values may be sent and summed in bfloat16 or wider, within the bound.
A program may use at most 128 MiB of HBM per device.

```python
import math
import jax
import jax.numpy as jnp
from jax import lax

TOPICS = 256
BLOCK = 128
SLOTS = 12
REMOTE = 3
SENDS = 4
ITERS = 2
BLOCKS_DEV = 32
SEED_DEV = 256
DOCS_DEV = 4096
DOCS = 524288
ROW_BLOCKS = 4096
SEEDS = 32768
N_GX = 4
N_GY = 32
DEVICES = 128


def draw_labels(key, part):
    first_key, second_key, third_key = jax.random.split(key, 3)
    block_level = jnp.exp(jax.random.uniform(first_key, (ROW_BLOCKS, 1, 1), jnp.float32, math.log(0.5), math.log(4.0)))
    topic_level = jnp.exp(jax.random.uniform(second_key, (1, 1, TOPICS), jnp.float32, math.log(0.5), math.log(6.0)))
    rough = jax.random.uniform(third_key, (ROW_BLOCKS, BLOCK, TOPICS), jnp.float32, 0.0, 1.0)
    values = block_level * topic_level * rough
    values = values.reshape(DOCS, TOPICS)
    top = jnp.max(values)
    return (values / top * 24.0).astype(jnp.float32)


def draw_weights(key, part):
    total = BLOCKS_DEV * DEVICES
    logs = jax.random.uniform(key, (total, SLOTS, BLOCK, BLOCK), jnp.float32, math.log(0.001), 0.0)
    values = jnp.exp(logs)
    return values.astype(jnp.bfloat16)


def draw_column_index(key, part):
    total = BLOCKS_DEV * DEVICES
    first_key, second_key, third_key = jax.random.split(key, 3)
    rows = jnp.arange(total, dtype=jnp.int32)
    device = rows // BLOCKS_DEV
    local = rows % BLOCKS_DEV
    outer = device // N_GY
    inner = device % N_GY
    local_cols = jax.random.randint(first_key, (total, SLOTS - REMOTE - 1), 0, BLOCKS_DEV, dtype=jnp.int32)
    offsets = jax.random.randint(second_key, (DEVICES,), 0, 4, dtype=jnp.int32)[device]
    position = local[:, None] * REMOTE + jnp.arange(REMOTE, dtype=jnp.int32)[None, :]
    direction = (position + offsets[:, None]) % 4
    present = jnp.where(direction == 0, inner[:, None] > 0, jnp.where(direction == 1, inner[:, None] < N_GY - 1, jnp.where(direction == 2, outer[:, None] > 0, outer[:, None] < N_GX - 1)))
    flipped = direction // 2 * 2 + 1 - direction % 2
    direction = jnp.where(present, direction, flipped)
    slot = jax.random.randint(third_key, (total, REMOTE), 0, SENDS, dtype=jnp.int32)
    remote = BLOCKS_DEV + direction * SENDS + slot
    return jnp.concatenate([local[:, None], local_cols, remote], axis=1).astype(jnp.int32)


def pick_blocks(subkey):
    return jax.random.permutation(subkey, BLOCKS_DEV)[:SENDS]


def draw_send_index(key, part):
    keys = jax.random.split(key, DEVICES * 4)
    chosen = jax.vmap(pick_blocks)(keys)
    return chosen.reshape(DEVICES, 4, SENDS).astype(jnp.int32)


def with_ends(drawn, key, low, top_value):
    extent = drawn.shape
    place = [jax.random.randint(jax.random.fold_in(key, axis), (), 0, extent[axis]) for axis in range(len(extent))]
    drawn = drawn.at[tuple(place)].set(low)
    longest = extent.index(max(extent))
    place[longest] = (place[longest] + 1) % extent[longest]
    return drawn.at[tuple(place)].set(top_value)


def setup_inputs(seed: int = 0) -> dict:
    streams_of = jax.random.split(jax.random.key(seed), 7)
    return {
        "labels": draw_labels(jax.random.fold_in(streams_of[6], 71), 0),
        "weights": draw_weights(jax.random.fold_in(streams_of[6], 71), 0),
        "column_index": draw_column_index(jax.random.fold_in(streams_of[6], 71), 0),
        "send_index": draw_send_index(jax.random.fold_in(streams_of[6], 71), 0),
        "seed_doc": with_ends(jax.random.randint(streams_of[4], (SEEDS,), 0, DOCS_DEV), jax.random.fold_in(streams_of[4], 1), 0, DOCS_DEV - 1).astype(jnp.int32),
        "seed_topic": with_ends(jax.random.randint(streams_of[5], (SEEDS,), 0, TOPICS), jax.random.fold_in(streams_of[5], 1), 0, TOPICS - 1).astype(jnp.int32),
    }


ALPHA = 0.99
GAIN = 1.0 / (1.0 - 0.99)

def shift_forward(values, axis):
    first = jnp.zeros_like(lax.slice_in_dim(values, 0, 1, axis=axis))
    rest = lax.slice_in_dim(values, 0, values.shape[axis] - 1, axis=axis)
    return jnp.concatenate([first, rest], axis=axis)

def shift_backward(values, axis):
    last = jnp.zeros_like(lax.slice_in_dim(values, 0, 1, axis=axis))
    rest = lax.slice_in_dim(values, 1, values.shape[axis], axis=axis)
    return jnp.concatenate([rest, last], axis=axis)

def degree_of(weight_part):
    return lax.optimization_barrier(jnp.sum(weight_part.astype(jnp.float32), axis=(1, 3)))

def select_sent(scaled_part, index_part):
    return scaled_part[index_part]

def block_products(items):
    weight_part, extended_part, column_part = items
    picked = extended_part[column_part]
    return jnp.einsum('rkij,rkjc->ric', weight_part.astype(jnp.float32), picked.astype(jnp.float32))

def reference(labels, weights, column_index, send_index, seed_doc, seed_topic):
    per_device = weights.reshape(DEVICES, BLOCKS_DEV, SLOTS, BLOCK, BLOCK)
    degree = lax.map(degree_of, per_device)
    scale = (1.0 / jnp.sqrt(degree)).reshape(DOCS, 1)
    owners = jnp.arange(SEEDS, dtype=jnp.int32) // SEED_DEV
    rows = owners * DOCS_DEV + seed_doc
    seeds = jnp.zeros((DOCS, TOPICS), jnp.float32).at[rows, seed_topic].add(GAIN)
    columns = column_index.reshape(DEVICES, BLOCKS_DEV, SLOTS)
    current = labels
    for iteration in range(ITERS):
        scaled = (scale * current).astype(jnp.bfloat16).reshape(DEVICES, BLOCKS_DEV, BLOCK, TOPICS)
        sent = jax.vmap(select_sent)(scaled, send_index)
        sent = sent.reshape(N_GX, N_GY, 4, SENDS, BLOCK, TOPICS)
        from_lower_inner = shift_forward(sent[:, :, 1], 1)
        from_upper_inner = shift_backward(sent[:, :, 0], 1)
        from_lower_outer = shift_forward(sent[:, :, 3], 0)
        from_upper_outer = shift_backward(sent[:, :, 2], 0)
        received = jnp.stack([from_lower_inner, from_upper_inner, from_lower_outer, from_upper_outer], axis=2)
        received = received.reshape(DEVICES, 4 * SENDS, BLOCK, TOPICS)
        extended = jnp.concatenate([scaled, received], axis=1)
        product = lax.map(block_products, (per_device, extended, columns))
        product = product.reshape(DOCS, TOPICS)
        current = ALPHA * scale * product + (1.0 - ALPHA) * seeds
    return current
```

```python
import functools

import jax
import jax.numpy as jnp
from jax import lax
from jax.experimental import pallas as pl
from jax.experimental.pallas import tpu as pltpu
from jax.sharding import PartitionSpec as P

ALPHA = 0.99
GAIN = 1.0 / (1.0 - 0.99)
SEED = (1.0 - ALPHA) * GAIN

MESH = pl.DeviceIdType.MESH
BF16 = jnp.bfloat16
F32 = jnp.float32
VMEM = pl.BlockSpec(memory_space=pltpu.VMEM)
SMEM = pl.BlockSpec(memory_space=pltpu.SMEM)
HBM = pl.BlockSpec(memory_space=pl.ANY)

EARLY = 8
CHUNK = 4
UNROLL = 8
DIRS = (2, 3, 0, 1)


def block_row(weight_ref, labels_ref, column_ref, row, first):
    count = weight_ref.shape[1]
    left = jnp.concatenate([weight_ref[row, k] for k in range(count)], axis=1)
    right = jnp.concatenate([labels_ref[column_ref[row, first + k]] for k in range(count)], axis=0)
    return jnp.dot(left, right, preferred_element_type=F32)


def doubled(scale):
    return jnp.concatenate([scale, scale], axis=1)


def spread_kernel(
    sizes,
    column_ref,
    send_ref,
    doc_ref,
    topic_ref,
    labels_hbm,
    weights_hbm,
    late_ref,
    next_ref,
    partial_ref,
    scale_ref,
    early_ref,
    labels_ref,
    now_ref,
    first_ref,
    count_ref,
    hot_ref,
    stage_a,
    stage_b,
    halo_a,
    halo_b,
    rows_out,
    rows_in,
    label_sem,
    early_sem,
    late_sem,
    send_a,
    recv_a,
    send_b,
    recv_b,
    send_s,
    recv_s,
):
    outer, inner = sizes
    blocks, block, topics = labels_hbm.shape
    sends = send_ref.shape[1]
    a, b = lax.axis_index("gx"), lax.axis_index("gy")
    has = [b > 0, b < inner - 1, a > 0, a < outer - 1]
    peer = [
        {"gx": a, "gy": b - 1},
        {"gx": a, "gy": b + 1},
        {"gx": a - 1, "gy": b},
        {"gx": a + 1, "gy": b},
    ]

    def remote(src, dst, send_sem, recv_sem, d):
        return pltpu.make_async_remote_copy(
            src_ref=src,
            dst_ref=dst,
            send_sem=send_sem,
            recv_sem=recv_sem,
            device_id=peer[d],
            device_id_type=MESH,
        )

    chunks = blocks // CHUNK
    label_copy = pltpu.make_async_copy(labels_hbm, labels_ref, label_sem)

    def early_copy(c):
        rows = pl.ds(c * CHUNK, CHUNK)
        return pltpu.make_async_copy(
            weights_hbm.at[rows, pl.ds(0, EARLY)], early_ref.at[rows], early_sem.at[c]
        )

    def late_copy(c):
        rows = pl.ds(c * CHUNK, CHUNK)
        late = weights_hbm.shape[1] - EARLY
        return pltpu.make_async_copy(
            weights_hbm.at[rows, pl.ds(EARLY, late)], late_ref.at[rows], late_sem.at[c]
        )

    label_copy.start()
    for c in range(2):
        early_copy(c).start()
        late_copy(c).start()

    barrier = pltpu.get_barrier_semaphore()
    for d in range(4):

        @pl.when(has[d])
        def _():
            pl.semaphore_signal(barrier, inc=1, device_id=peer[d], device_id_type=MESH)

    seeds = doc_ref.shape[1]
    wanted = jnp.broadcast_to(topic_ref[...], (topics, seeds))
    ours = lax.broadcasted_iota(jnp.int32, (topics, seeds), 0)
    hot_ref[...] = jnp.where(wanted == ours, 1.0, 0.0).astype(F32).T.astype(BF16)

    def count_rows(g, carry):
        for u in range(CHUNK):
            r = g * CHUNK + u
            docs = lax.broadcasted_iota(jnp.int32, (block, seeds), 0) + r * block
            hot = jnp.where(docs == jnp.broadcast_to(doc_ref[...], (block, seeds)), 1.0, 0.0)
            found = jnp.dot(hot.astype(BF16), hot_ref[...], preferred_element_type=F32)
            count_ref[r] = found.astype(BF16)
        return carry

    lax.fori_loop(0, chunks, count_rows, 0)

    pl.semaphore_wait(barrier, sum(jnp.where(h, 1, 0) for h in has))

    label_copy.wait()
    for c in range(2, chunks):
        early_copy(c).start()
        late_copy(c).start()
    for d in DIRS:
        for s in range(sends):
            stage_a[d, s] = labels_ref[send_ref[d, s]].astype(BF16)

        @pl.when(has[d])
        def _():
            remote(stage_a.at[d], halo_a.at[d ^ 1], send_a.at[d], recv_a.at[d ^ 1], d).start()

    def degree_rows(c, carry):
        early_copy(c).wait()
        late_copy(c).wait()
        for u in range(CHUNK):
            r = c * CHUNK + u
            total = early_ref[r, 0].astype(F32)
            for k in range(1, EARLY):
                total = total + early_ref[r, k].astype(F32)
            for k in range(late_ref.shape[1]):
                total = total + late_ref[r, k].astype(F32)
            degree = jnp.sum(total, axis=1, keepdims=True)
            scale = jnp.broadcast_to(1.0 / jnp.sqrt(degree), (block, block))
            scale_ref[r] = scale
            now_ref[r] = (doubled(scale) * labels_ref[r]).astype(BF16)
        return carry

    lax.fori_loop(0, chunks, degree_rows, 0)

    lanes = lax.broadcasted_iota(jnp.int32, (block, block), 1)
    columns = jnp.zeros((block, block), F32)
    for d in range(4):
        for s in range(sends):
            columns = jnp.where(lanes == d * 8 + s, scale_ref[send_ref[d, s]], columns)
    rows = columns.T
    for d in DIRS:
        rows_out[d] = rows[d * 8 : d * 8 + 8]

        @pl.when(has[d])
        def _():
            remote(rows_out.at[d], rows_in.at[d ^ 1], send_s.at[d], recv_s.at[d ^ 1], d).start()

    def first_early(g, carry):
        for u in range(UNROLL):
            r = g * UNROLL + u
            first_ref[r] = block_row(early_ref, now_ref, column_ref, r, 0)
        return carry

    lax.fori_loop(0, blocks // UNROLL, first_early, 0)

    for d in range(4):

        @pl.when(has[d])
        def _():
            remote(stage_a.at[d], halo_a.at[d], send_a.at[d], recv_a.at[d], d).wait_recv()
            remote(rows_out.at[d], rows_in.at[d], send_s.at[d], recv_s.at[d], d).wait_recv()

        @pl.when(jnp.logical_not(has[d]))
        def _():
            rows_in[d] = jnp.zeros(rows_in.shape[1:], F32)
            halo_a[d] = jnp.zeros(halo_a.shape[1:], BF16)

    taken = jnp.concatenate(
        [rows_in[d] for d in range(4)] + [jnp.zeros((block - 32, block), F32)], axis=0
    )
    scales = taken.T
    for d in range(4):
        for s in range(sends):
            scale = jnp.broadcast_to(scales[:, d * 8 + s : d * 8 + s + 1], (block, topics))
            now_ref[blocks + d * sends + s] = (scale * halo_a[d, s].astype(F32)).astype(BF16)

    def next_scaled(r):
        scale = doubled(scale_ref[r])
        product = first_ref[r] + block_row(late_ref, now_ref, column_ref, r, EARLY)
        current = ALPHA * scale * product + SEED * count_ref[r].astype(F32)
        return (scale * current).astype(BF16)

    def sent_rows(s, carry):
        for d in DIRS:
            stage_b[d, s] = next_scaled(send_ref[d, s])
        for d in DIRS:

            @pl.when(has[d])
            def _():
                remote(
                    stage_b.at[d, s], halo_b.at[d ^ 1, s], send_b.at[d, s], recv_b.at[d ^ 1, s], d
                ).start()

        return carry

    lax.fori_loop(0, sends, sent_rows, 0)

    def first_late(g, carry):
        for u in range(UNROLL):
            r = g * UNROLL + u
            next_ref[r] = next_scaled(r)
        return carry

    lax.fori_loop(0, blocks // UNROLL, first_late, 0)

    def second_early(g, carry):
        for u in range(UNROLL):
            r = g * UNROLL + u
            product = block_row(early_ref, next_ref, column_ref, r, 0)
            scale = doubled(scale_ref[r])
            partial_ref[r] = ALPHA * scale * product + SEED * count_ref[r].astype(F32)
        return carry

    lax.fori_loop(0, blocks // UNROLL, second_early, 0)

    for d in range(4):

        @pl.when(has[d])
        def _():
            for s in range(sends):
                remote(
                    stage_b.at[d, s], halo_b.at[d, s], send_b.at[d, s], recv_b.at[d, s], d
                ).wait_recv()

        @pl.when(jnp.logical_not(has[d]))
        def _():
            halo_b[d] = jnp.zeros(halo_b.shape[1:], BF16)

    for d in range(4):
        for s in range(sends):
            next_ref[blocks + d * sends + s] = halo_b[d, s]

    for d in range(4):

        @pl.when(has[d])
        def _():
            remote(stage_a.at[d], halo_a.at[d], send_a.at[d], recv_a.at[d], d).wait_send()
            remote(rows_out.at[d], rows_in.at[d], send_s.at[d], recv_s.at[d], d).wait_send()
            for s in range(sends):
                remote(
                    stage_b.at[d, s], halo_b.at[d, s], send_b.at[d, s], recv_b.at[d, s], d
                ).wait_send()


def finish_kernel(column_ref, late_ref, next_ref, partial_ref, scale_ref, out_ref):
    g = pl.program_id(0)
    for u in range(out_ref.shape[0]):
        r = g * out_ref.shape[0] + u
        product = block_row(late_ref, next_ref, column_ref, r, EARLY)
        out_ref[u] = partial_ref[r] + ALPHA * doubled(scale_ref[r]) * product


def local(sizes, labels, weights, column_index, send_index, seed_doc, seed_topic):
    blocks, slots, block, _ = weights.shape
    topics = labels.shape[1]
    dirs, sends = send_index.shape[1:]
    halo = dirs * sends
    chunks = blocks // CHUNK
    late, following, partial, scale = pl.pallas_call(
        functools.partial(spread_kernel, sizes),
        out_shape=(
            jax.ShapeDtypeStruct((blocks, slots - EARLY, block, block), BF16),
            jax.ShapeDtypeStruct((blocks + halo, block, topics), BF16),
            jax.ShapeDtypeStruct((blocks, block, topics), F32),
            jax.ShapeDtypeStruct((blocks, block, block), F32),
        ),
        in_specs=[SMEM, SMEM, VMEM, VMEM, HBM, HBM],
        out_specs=(VMEM, VMEM, VMEM, VMEM),
        scratch_shapes=[
            pltpu.VMEM((blocks, EARLY, block, block), BF16),
            pltpu.VMEM((blocks, block, topics), F32),
            pltpu.VMEM((blocks + halo, block, topics), BF16),
            pltpu.VMEM((blocks, block, topics), F32),
            pltpu.VMEM((blocks, block, topics), BF16),
            pltpu.VMEM((seed_doc.shape[0], topics), BF16),
            pltpu.VMEM((dirs, sends, block, topics), BF16),
            pltpu.VMEM((dirs, sends, block, topics), BF16),
            pltpu.VMEM((dirs, sends, block, topics), BF16),
            pltpu.VMEM((dirs, sends, block, topics), BF16),
            pltpu.VMEM((dirs, 8, block), F32),
            pltpu.VMEM((dirs, 8, block), F32),
            pltpu.SemaphoreType.DMA,
            pltpu.SemaphoreType.DMA((chunks,)),
            pltpu.SemaphoreType.DMA((chunks,)),
            pltpu.SemaphoreType.DMA((dirs,)),
            pltpu.SemaphoreType.DMA((dirs,)),
            pltpu.SemaphoreType.DMA((dirs, sends)),
            pltpu.SemaphoreType.DMA((dirs, sends)),
            pltpu.SemaphoreType.DMA((dirs,)),
            pltpu.SemaphoreType.DMA((dirs,)),
        ],
        compiler_params=pltpu.CompilerParams(
            collective_id=0, has_side_effects=True, vmem_limit_bytes=38 << 20
        ),
        name="spread",
    )(
        column_index,
        send_index.reshape(dirs, sends),
        seed_doc.reshape(1, -1),
        seed_topic.reshape(1, -1),
        labels.reshape(blocks, block, topics),
        weights,
    )
    out = pl.pallas_call(
        finish_kernel,
        grid=(blocks // UNROLL,),
        out_shape=jax.ShapeDtypeStruct((blocks, block, topics), F32),
        in_specs=[SMEM, VMEM, VMEM, VMEM, VMEM],
        out_specs=pl.BlockSpec((UNROLL, block, topics), lambda g: (g, 0, 0)),
        compiler_params=pltpu.CompilerParams(vmem_limit_bytes=30 << 20),
        name="finish",
    )(column_index, late, following, partial, scale)
    return out.reshape(blocks * block, topics)


def solution(mesh):
    sizes = (mesh.shape["gx"], mesh.shape["gy"])
    parts = P(("gx", "gy"))
    return jax.shard_map(
        functools.partial(local, sizes),
        mesh=mesh,
        in_specs=(parts,) * 6,
        out_specs=parts,
        check_vma=False,
    )
```

```python
import functools

import jax
import jax.numpy as jnp
from jax import lax
from jax.experimental import pallas as pl
from jax.experimental.pallas import tpu as pltpu
from jax.sharding import PartitionSpec as P

ALPHA = 0.99
GAIN = 1.0 / (1.0 - 0.99)
SEED = (1.0 - ALPHA) * GAIN

MESH = pl.DeviceIdType.MESH
BF16 = jnp.bfloat16
F32 = jnp.float32
VMEM = pl.BlockSpec(memory_space=pltpu.VMEM)
HBM = pl.BlockSpec(memory_space=pl.ANY)

EARLY = 8
CHUNK = 4
FIRST = 1
WIDE = 16
GROUP = 4
DIRS = (2, 3, 0, 1)


def block_row(parts, labels_ref, table_ref, row):
    left, right = [], []
    for weight_ref, first in parts:
        for k in range(weight_ref.shape[1]):
            left.append(weight_ref[row, k])
            right.append(labels_ref[table_ref[first + k, row]])
    return jnp.dot(
        jnp.concatenate(left, axis=1),
        jnp.concatenate(right, axis=0),
        preferred_element_type=F32,
    )


def doubled(scale):
    return jnp.concatenate([scale, scale], axis=1)


def spread_kernel(
    sizes,
    whole_ref,
    labels_hbm,
    weights_hbm,
    late_ref,
    next_ref,
    partial_ref,
    scale_ref,
    table_ref,
    early_ref,
    labels_ref,
    now_ref,
    first_ref,
    count_ref,
    hot_ref,
    stage_a,
    stage_b,
    halo_a,
    mine_ref,
    rows_out,
    rows_in,
    table_sem,
    label_sem,
    early_sem,
    late_sem,
    send_a,
    recv_a,
    send_b,
    recv_b,
    send_s,
    recv_s,
):
    outer, inner = sizes
    blocks, block, topics = labels_hbm.shape
    seeds = whole_ref.shape[1]
    sends = halo_a.shape[1]
    slots = weights_hbm.shape[1]
    a, b = lax.axis_index("gx"), lax.axis_index("gy")
    has = [b > 0, b < inner - 1, a > 0, a < outer - 1]
    peer = [
        {"gx": a, "gy": b - 1},
        {"gx": a, "gy": b + 1},
        {"gx": a - 1, "gy": b},
        {"gx": a + 1, "gy": b},
    ]

    def remote(src, dst, send_sem, recv_sem, d):
        return pltpu.make_async_remote_copy(
            src_ref=src,
            dst_ref=dst,
            send_sem=send_sem,
            recv_sem=recv_sem,
            device_id=peer[d],
            device_id_type=MESH,
        )

    chunks = blocks // CHUNK
    label_copy = pltpu.make_async_copy(labels_hbm, labels_ref, label_sem)

    def early_copy(c):
        rows = pl.ds(c * CHUNK, CHUNK)
        return pltpu.make_async_copy(
            weights_hbm.at[rows, pl.ds(0, EARLY)], early_ref.at[rows], early_sem.at[c]
        )

    def late_copy(c):
        rows = pl.ds(c * CHUNK, CHUNK)
        late = weights_hbm.shape[1] - EARLY
        return pltpu.make_async_copy(
            weights_hbm.at[rows, pl.ds(EARLY, late)], late_ref.at[rows], late_sem.at[c]
        )

    label_copy.start()
    table_copy = pltpu.make_async_copy(whole_ref.at[0:16, 0:128], table_ref, table_sem)
    table_copy.start()
    for c in range(FIRST):
        early_copy(c).start()
        late_copy(c).start()

    barrier = pltpu.get_barrier_semaphore()
    for d in range(4):

        @pl.when(has[d])
        def _():
            pl.semaphore_signal(barrier, inc=1, device_id=peer[d], device_id_type=MESH)

    pl.semaphore_wait(barrier, sum(jnp.where(h, 1, 0) for h in has))

    table_copy.wait()
    label_copy.wait()
    for c in range(FIRST, chunks):
        early_copy(c).start()
        late_copy(c).start()
    for d in DIRS:
        for s in range(sends):
            stage_a[d, s] = labels_ref[table_ref[slots + d, s]].astype(BF16)

        @pl.when(has[d])
        def _():
            remote(stage_a.at[d], halo_a.at[d ^ 1], send_a.at[d], recv_a.at[d ^ 1], d).start()

    wanted = jnp.broadcast_to(whole_ref[17:18], (topics, seeds))
    ours = lax.broadcasted_iota(jnp.int32, (topics, seeds), 0)
    hot_ref[...] = jnp.where(wanted == ours, 1.0, 0.0).astype(F32).T.astype(BF16)

    wanted_docs = jnp.broadcast_to(whole_ref[16:17], (block, seeds))

    def count_rows(g, carry):
        for u in range(CHUNK):
            r = g * CHUNK + u
            docs = lax.broadcasted_iota(jnp.int32, (block, seeds), 0) + r * block
            hot = jnp.where(docs == wanted_docs, 1.0, 0.0)
            found = jnp.dot(hot.astype(BF16), hot_ref[...], preferred_element_type=F32)
            count_ref[r] = found.astype(BF16)
        return carry

    lax.fori_loop(0, chunks, count_rows, 0)

    def degree_rows(c, carry):
        early_copy(c).wait()
        late_copy(c).wait()
        for u in range(CHUNK):
            r = c * CHUNK + u
            total = early_ref[r, 0].astype(F32)
            for k in range(1, EARLY):
                total = total + early_ref[r, k].astype(F32)
            for k in range(late_ref.shape[1]):
                total = total + late_ref[r, k].astype(F32)
            degree = jnp.sum(total, axis=1, keepdims=True)
            scale = jnp.broadcast_to(1.0 / jnp.sqrt(degree), (block, block))
            scale_ref[r] = scale
            now_ref[r] = (doubled(scale) * labels_ref[r]).astype(BF16)
        return carry

    lax.fori_loop(0, chunks, degree_rows, 0)

    lanes = lax.broadcasted_iota(jnp.int32, (block, block), 1)
    columns = jnp.zeros((block, block), F32)
    for d in range(4):
        for s in range(sends):
            columns = jnp.where(lanes == d * 8 + s, scale_ref[table_ref[slots + d, s]], columns)
    rows = columns.T
    for d in DIRS:
        rows_out[d] = rows[d * 8 : d * 8 + 8]

        @pl.when(has[d])
        def _():
            remote(rows_out.at[d], rows_in.at[d ^ 1], send_s.at[d], recv_s.at[d ^ 1], d).start()

    def sent_early(g, carry):
        for u in range(2):
            for d in DIRS:
                i = g * 2 + u
                row = table_ref[slots + d, i]
                first_ref[d, i] = block_row([(early_ref, 0)], now_ref, table_ref, row)
        return carry

    lax.fori_loop(0, sends // 2, sent_early, 0)

    for d in range(4):

        @pl.when(has[d])
        def _():
            remote(rows_out.at[d], rows_in.at[d], send_s.at[d], recv_s.at[d], d).wait_recv()

        @pl.when(jnp.logical_not(has[d]))
        def _():
            rows_in[d] = jnp.zeros(rows_in.shape[1:], F32)

    taken = jnp.concatenate(
        [rows_in[d] for d in range(4)] + [jnp.zeros((block - 32, block), F32)], axis=0
    )
    scales = taken.T
    for d in (0, 1, 2, 3):

        @pl.when(has[d])
        def _():
            remote(stage_a.at[d], halo_a.at[d], send_a.at[d], recv_a.at[d], d).wait_recv()

        @pl.when(jnp.logical_not(has[d]))
        def _():
            halo_a[d] = jnp.zeros(halo_a.shape[1:], BF16)

        for s in range(sends):
            scale = jnp.broadcast_to(scales[:, d * 8 + s : d * 8 + s + 1], (block, topics))
            now_ref[blocks + d * sends + s] = (scale * halo_a[d, s].astype(F32)).astype(BF16)

    def next_scaled(r, product):
        scale = doubled(scale_ref[r])
        current = ALPHA * scale * product + SEED * count_ref[r].astype(F32)
        return (scale * current).astype(BF16)

    def halo_copy(d, s):
        block_at = blocks + (d ^ 1) * sends + s
        return remote(
            stage_b.at[d, s], next_ref.at[block_at], send_b.at[d, s], recv_b.at[d ^ 1, s], d
        )

    def halo_arrival(d, s):
        block_at = blocks + d * sends + s
        return remote(
            stage_b.at[d, s], next_ref.at[block_at], send_b.at[d, s], recv_b.at[d, s], d
        )

    for s in range(sends):
        for d in DIRS:
            row = table_ref[slots + d, s]
            late = block_row([(late_ref, EARLY)], now_ref, table_ref, row)
            stage_b[d, s] = next_scaled(row, first_ref[d, s] + late)
        for d in DIRS:

            @pl.when(has[d])
            def _():
                halo_copy(d, s).start()

    def first_rows(g, carry):
        for u in range(WIDE):
            r = g * WIDE + u
            parts = [(early_ref, 0), (late_ref, EARLY)]
            scaled = next_scaled(r, block_row(parts, now_ref, table_ref, r))
            mine_ref[r] = scaled
            next_ref[r] = scaled
        return carry

    lax.fori_loop(0, blocks // WIDE, first_rows, 0)

    def second_early(g, carry):
        for u in range(WIDE):
            r = g * WIDE + u
            product = block_row([(early_ref, 0)], mine_ref, table_ref, r)
            scale = doubled(scale_ref[r])
            partial_ref[r] = ALPHA * scale * product + SEED * count_ref[r].astype(F32)
        return carry

    lax.fori_loop(0, blocks // WIDE, second_early, 0)

    for d in range(4):

        @pl.when(has[d])
        def _():
            for s in range(sends):
                halo_arrival(d, s).wait_recv()

        @pl.when(jnp.logical_not(has[d]))
        def _():
            for s in range(sends):
                next_ref[blocks + d * sends + s] = jnp.zeros((block, topics), BF16)

    for d in range(4):

        @pl.when(has[d])
        def _():
            remote(stage_a.at[d], halo_a.at[d], send_a.at[d], recv_a.at[d], d).wait_send()
            remote(rows_out.at[d], rows_in.at[d], send_s.at[d], recv_s.at[d], d).wait_send()
            for s in range(sends):
                halo_arrival(d, s).wait_send()


def finish_kernel(
    whole_ref, late_ref, next_ref, partial_ref, scale_ref, out_hbm, table_ref, out_ref, sem, sems
):
    blocks = out_ref.shape[0]
    table_copy = pltpu.make_async_copy(whole_ref.at[0:16, 0:128], table_ref, sem)
    table_copy.start()
    table_copy.wait()

    def write(g):
        rows = pl.ds(g * GROUP, GROUP)
        return pltpu.make_async_copy(out_ref.at[rows], out_hbm.at[rows], sems.at[g])

    def finish_rows(t, carry):
        for q in range(WIDE // GROUP):
            g = t * (WIDE // GROUP) + q
            for u in range(GROUP):
                r = g * GROUP + u
                product = block_row([(late_ref, EARLY)], next_ref, table_ref, r)
                out_ref[r] = partial_ref[r] + ALPHA * doubled(scale_ref[r]) * product
            write(g).start()
        return carry

    lax.fori_loop(0, blocks // WIDE, finish_rows, 0)
    for g in range(blocks // GROUP):
        write(g).wait()


def placed(rows, first, height, width):
    return jnp.pad(rows, ((first, height - first - rows.shape[0]), (0, width - rows.shape[1])))


def local(sizes, labels, weights, column_index, send_index, seed_doc, seed_topic):
    blocks, slots, block, _ = weights.shape
    topics = labels.shape[1]
    dirs, sends = send_index.shape[1:]
    halo = dirs * sends
    chunks = blocks // CHUNK
    seeds = seed_doc.shape[0]
    put = functools.partial(placed, height=24, width=seeds)
    table = put(column_index.T, 0) + put(send_index.reshape(dirs, sends), slots)
    table += put(seed_doc.reshape(1, seeds), 16) + put(seed_topic.reshape(1, seeds), 17)
    late, following, partial, scale = pl.pallas_call(
        functools.partial(spread_kernel, sizes),
        out_shape=(
            jax.ShapeDtypeStruct((blocks, slots - EARLY, block, block), BF16),
            jax.ShapeDtypeStruct((blocks + halo, block, topics), BF16),
            jax.ShapeDtypeStruct((blocks, block, topics), F32),
            jax.ShapeDtypeStruct((blocks, block, block), F32),
        ),
        in_specs=[VMEM, HBM, HBM],
        out_specs=(VMEM, VMEM, VMEM, VMEM),
        scratch_shapes=[
            pltpu.SMEM((16, 128), jnp.int32),
            pltpu.VMEM((blocks, EARLY, block, block), BF16),
            pltpu.VMEM((blocks, block, topics), F32),
            pltpu.VMEM((blocks + halo, block, topics), BF16),
            pltpu.VMEM((dirs, sends, block, topics), F32),
            pltpu.VMEM((blocks, block, topics), BF16),
            pltpu.VMEM((seed_doc.shape[0], topics), BF16),
            pltpu.VMEM((dirs, sends, block, topics), BF16),
            pltpu.VMEM((dirs, sends, block, topics), BF16),
            pltpu.VMEM((dirs, sends, block, topics), BF16),
            pltpu.VMEM((blocks, block, topics), BF16),
            pltpu.VMEM((dirs, 8, block), F32),
            pltpu.VMEM((dirs, 8, block), F32),
            pltpu.SemaphoreType.DMA,
            pltpu.SemaphoreType.DMA,
            pltpu.SemaphoreType.DMA((chunks,)),
            pltpu.SemaphoreType.DMA((chunks,)),
            pltpu.SemaphoreType.DMA((dirs,)),
            pltpu.SemaphoreType.DMA((dirs,)),
            pltpu.SemaphoreType.DMA((dirs, sends)),
            pltpu.SemaphoreType.DMA((dirs, sends)),
            pltpu.SemaphoreType.DMA((dirs,)),
            pltpu.SemaphoreType.DMA((dirs,)),
        ],
        compiler_params=pltpu.CompilerParams(
            collective_id=0, has_side_effects=True, vmem_limit_bytes=38 << 20
        ),
        name="spread",
    )(
        table,
        labels.reshape(blocks, block, topics),
        weights,
    )
    out = pl.pallas_call(
        finish_kernel,
        out_shape=jax.ShapeDtypeStruct((blocks, block, topics), F32),
        in_specs=[VMEM, VMEM, VMEM, VMEM, VMEM],
        out_specs=HBM,
        scratch_shapes=[
            pltpu.SMEM((16, 128), jnp.int32),
            pltpu.VMEM((blocks, block, topics), F32),
            pltpu.SemaphoreType.DMA,
            pltpu.SemaphoreType.DMA((blocks // GROUP,)),
        ],
        compiler_params=pltpu.CompilerParams(vmem_limit_bytes=30 << 20),
        name="finish",
    )(table, late, following, partial, scale)
    return out.reshape(blocks * block, topics)


def solution(mesh):
    sizes = (mesh.shape["gx"], mesh.shape["gy"])
    parts = P(("gx", "gy"))
    return jax.shard_map(
        functools.partial(local, sizes),
        mesh=mesh,
        in_specs=(parts,) * 6,
        out_specs=parts,
        check_vma=False,
    )
```

```python
import functools

import jax
import jax.numpy as jnp
from jax import lax
from jax.experimental import pallas as pl
from jax.experimental.pallas import tpu as pltpu
from jax.sharding import PartitionSpec as P

ALPHA = 0.99
GAIN = 1.0 / (1.0 - 0.99)
SEED = (1.0 - ALPHA) * GAIN

MESH = pl.DeviceIdType.MESH
BF16 = jnp.bfloat16
F32 = jnp.float32
VMEM = pl.BlockSpec(memory_space=pltpu.VMEM)
HBM = pl.BlockSpec(memory_space=pl.ANY)

EARLY = 8
CHUNK = 4
FILLED = 16
WIDE = 16
GROUP = 4
DIRS = (2, 3, 0, 1)


def block_row(parts, labels_ref, table_ref, row):
    left, right = [], []
    for weight_ref, first in parts:
        for k in range(weight_ref.shape[1]):
            left.append(weight_ref[row, k])
            right.append(labels_ref[table_ref[first + k, row]])
    return jnp.dot(
        jnp.concatenate(left, axis=1),
        jnp.concatenate(right, axis=0),
        preferred_element_type=F32,
    )


def doubled(scale):
    return jnp.concatenate([scale, scale], axis=1)


def spread_kernel(
    sizes,
    whole_ref,
    labels_hbm,
    weights_hbm,
    late_ref,
    next_ref,
    partial_ref,
    scale_ref,
    table_ref,
    early_ref,
    labels_ref,
    now_ref,
    first_ref,
    fill_ref,
    count_ref,
    hot_ref,
    stage_a,
    stage_b,
    halo_a,
    mine_ref,
    rows_out,
    rows_in,
    table_sem,
    label_sem,
    early_sem,
    late_sem,
    send_a,
    recv_a,
    send_b,
    recv_b,
    send_s,
    recv_s,
):
    outer, inner = sizes
    blocks, block, topics = labels_hbm.shape
    seeds = whole_ref.shape[1]
    sends = halo_a.shape[1]
    slots = weights_hbm.shape[1]
    a, b = lax.axis_index("gx"), lax.axis_index("gy")
    has = [b > 0, b < inner - 1, a > 0, a < outer - 1]
    peer = [
        {"gx": a, "gy": b - 1},
        {"gx": a, "gy": b + 1},
        {"gx": a - 1, "gy": b},
        {"gx": a + 1, "gy": b},
    ]

    def remote(src, dst, send_sem, recv_sem, d):
        return pltpu.make_async_remote_copy(
            src_ref=src,
            dst_ref=dst,
            send_sem=send_sem,
            recv_sem=recv_sem,
            device_id=peer[d],
            device_id_type=MESH,
        )

    chunks = blocks // CHUNK
    label_copy = pltpu.make_async_copy(labels_hbm, labels_ref, label_sem)

    def early_copy(c):
        rows = pl.ds(c * CHUNK, CHUNK)
        return pltpu.make_async_copy(
            weights_hbm.at[rows, pl.ds(0, EARLY)], early_ref.at[rows], early_sem.at[c]
        )

    def late_copy(c):
        rows = pl.ds(c * CHUNK, CHUNK)
        late = weights_hbm.shape[1] - EARLY
        return pltpu.make_async_copy(
            weights_hbm.at[rows, pl.ds(EARLY, late)], late_ref.at[rows], late_sem.at[c]
        )

    label_copy.start()
    table_copy = pltpu.make_async_copy(whole_ref.at[0:16, 0:128], table_ref, table_sem)
    table_copy.start()
    for c in range(chunks):
        early_copy(c).start(priority=1)
        late_copy(c).start(priority=1)

    barrier = pltpu.get_barrier_semaphore()
    for d in range(4):

        @pl.when(has[d])
        def _():
            pl.semaphore_signal(barrier, inc=1, device_id=peer[d], device_id_type=MESH)

    pl.semaphore_wait(barrier, sum(jnp.where(h, 1, 0) for h in has))

    table_copy.wait()
    label_copy.wait()
    for d in DIRS:
        for s in range(sends):
            stage_a[d, s] = labels_ref[table_ref[slots + d, s]].astype(BF16)

        @pl.when(has[d])
        def _():
            remote(stage_a.at[d], halo_a.at[d ^ 1], send_a.at[d], recv_a.at[d ^ 1], d).start()

    wanted = jnp.broadcast_to(whole_ref[17:18], (topics, seeds))
    ours = lax.broadcasted_iota(jnp.int32, (topics, seeds), 0)
    hot_ref[...] = jnp.where(wanted == ours, 1.0, 0.0).astype(F32).T.astype(BF16)

    wanted_docs = jnp.broadcast_to(whole_ref[16:17], (block, seeds))

    def count_rows(g, carry):
        for u in range(CHUNK):
            r = g * CHUNK + u
            docs = lax.broadcasted_iota(jnp.int32, (block, seeds), 0) + r * block
            hot = jnp.where(docs == wanted_docs, 1.0, 0.0)
            found = jnp.dot(hot.astype(BF16), hot_ref[...], preferred_element_type=F32)
            count_ref[r] = found.astype(BF16)
        return carry

    lax.fori_loop(0, chunks, count_rows, 0)

    def degree_rows(c, carry):
        early_copy(c).wait()
        late_copy(c).wait()
        for u in range(CHUNK):
            r = c * CHUNK + u
            total = early_ref[r, 0].astype(F32)
            for k in range(1, EARLY):
                total = total + early_ref[r, k].astype(F32)
            for k in range(late_ref.shape[1]):
                total = total + late_ref[r, k].astype(F32)
            degree = jnp.sum(total, axis=1, keepdims=True)
            scale = jnp.broadcast_to(1.0 / jnp.sqrt(degree), (block, block))
            scale_ref[r] = scale
            now_ref[r] = (doubled(scale) * labels_ref[r]).astype(BF16)
        return carry

    lax.fori_loop(0, chunks, degree_rows, 0)

    lanes = lax.broadcasted_iota(jnp.int32, (block, block), 1)
    columns = jnp.zeros((block, block), F32)
    for d in range(4):
        for s in range(sends):
            columns = jnp.where(lanes == d * 8 + s, scale_ref[table_ref[slots + d, s]], columns)
    rows = columns.T
    for d in DIRS:
        rows_out[d] = rows[d * 8 : d * 8 + 8]

        @pl.when(has[d])
        def _():
            remote(rows_out.at[d], rows_in.at[d ^ 1], send_s.at[d], recv_s.at[d ^ 1], d).start()

    def sent_early(g, carry):
        for u in range(2):
            for d in DIRS:
                i = g * 2 + u
                row = table_ref[slots + d, i]
                first_ref[d, i] = block_row([(early_ref, 0)], now_ref, table_ref, row)
        return carry

    lax.fori_loop(0, sends // 2, sent_early, 0)

    def fill_rows(g, carry):
        for u in range(WIDE):
            r = g * WIDE + u
            fill_ref[r] = block_row([(early_ref, 0)], now_ref, table_ref, r)
        return carry

    lax.fori_loop(0, FILLED // WIDE, fill_rows, 0)

    for d in range(4):

        @pl.when(has[d])
        def _():
            remote(rows_out.at[d], rows_in.at[d], send_s.at[d], recv_s.at[d], d).wait_recv()

        @pl.when(jnp.logical_not(has[d]))
        def _():
            rows_in[d] = jnp.zeros(rows_in.shape[1:], F32)

    taken = jnp.concatenate(
        [rows_in[d] for d in range(4)] + [jnp.zeros((block - 32, block), F32)], axis=0
    )
    scales = taken.T
    for d in (0, 1, 2, 3):

        @pl.when(has[d])
        def _():
            remote(stage_a.at[d], halo_a.at[d], send_a.at[d], recv_a.at[d], d).wait_recv()

        @pl.when(jnp.logical_not(has[d]))
        def _():
            halo_a[d] = jnp.zeros(halo_a.shape[1:], BF16)

        for s in range(sends):
            scale = jnp.broadcast_to(scales[:, d * 8 + s : d * 8 + s + 1], (block, topics))
            now_ref[blocks + d * sends + s] = (scale * halo_a[d, s].astype(F32)).astype(BF16)

    def next_scaled(r, product):
        scale = doubled(scale_ref[r])
        current = ALPHA * scale * product + SEED * count_ref[r].astype(F32)
        return (scale * current).astype(BF16)

    def halo_copy(d, s):
        block_at = blocks + (d ^ 1) * sends + s
        return remote(
            stage_b.at[d, s], next_ref.at[block_at], send_b.at[d, s], recv_b.at[d ^ 1, s], d
        )

    def halo_arrival(d, s):
        block_at = blocks + d * sends + s
        return remote(
            stage_b.at[d, s], next_ref.at[block_at], send_b.at[d, s], recv_b.at[d, s], d
        )

    for s in range(sends):
        for d in DIRS:
            row = table_ref[slots + d, s]
            late = block_row([(late_ref, EARLY)], now_ref, table_ref, row)
            stage_b[d, s] = next_scaled(row, first_ref[d, s] + late)
        for d in DIRS:

            @pl.when(has[d])
            def _():
                halo_copy(d, s).start()

    def keep(r, product):
        scaled = next_scaled(r, product)
        mine_ref[r] = scaled
        next_ref[r] = scaled

    def filled_rows(g, carry):
        for u in range(WIDE):
            r = g * WIDE + u
            keep(r, fill_ref[r] + block_row([(late_ref, EARLY)], now_ref, table_ref, r))
        return carry

    lax.fori_loop(0, FILLED // WIDE, filled_rows, 0)

    def first_rows(g, carry):
        for u in range(WIDE):
            r = g * WIDE + u
            parts = [(early_ref, 0), (late_ref, EARLY)]
            keep(r, block_row(parts, now_ref, table_ref, r))
        return carry

    lax.fori_loop(FILLED // WIDE, blocks // WIDE, first_rows, 0)

    def second_early(g, carry):
        for u in range(WIDE):
            r = g * WIDE + u
            product = block_row([(early_ref, 0)], mine_ref, table_ref, r)
            scale = doubled(scale_ref[r])
            partial_ref[r] = ALPHA * scale * product + SEED * count_ref[r].astype(F32)
        return carry

    lax.fori_loop(0, blocks // WIDE, second_early, 0)

    for d in range(4):

        @pl.when(has[d])
        def _():
            for s in range(sends):
                halo_arrival(d, s).wait_recv()

        @pl.when(jnp.logical_not(has[d]))
        def _():
            for s in range(sends):
                next_ref[blocks + d * sends + s] = jnp.zeros((block, topics), BF16)

    for d in range(4):

        @pl.when(has[d])
        def _():
            remote(stage_a.at[d], halo_a.at[d], send_a.at[d], recv_a.at[d], d).wait_send()
            remote(rows_out.at[d], rows_in.at[d], send_s.at[d], recv_s.at[d], d).wait_send()
            for s in range(sends):
                halo_arrival(d, s).wait_send()


def finish_kernel(
    whole_ref, late_ref, next_ref, partial_ref, scale_ref, out_hbm, table_ref, out_ref, sem, sems
):
    blocks = out_ref.shape[0]
    table_copy = pltpu.make_async_copy(whole_ref.at[0:16, 0:128], table_ref, sem)
    table_copy.start()
    table_copy.wait()

    def write(g):
        rows = pl.ds(g * GROUP, GROUP)
        return pltpu.make_async_copy(out_ref.at[rows], out_hbm.at[rows], sems.at[g])

    def finish_rows(t, carry):
        for q in range(WIDE // GROUP):
            g = t * (WIDE // GROUP) + q
            for u in range(GROUP):
                r = g * GROUP + u
                product = block_row([(late_ref, EARLY)], next_ref, table_ref, r)
                out_ref[r] = partial_ref[r] + ALPHA * doubled(scale_ref[r]) * product
            write(g).start()
        return carry

    lax.fori_loop(0, blocks // WIDE, finish_rows, 0)
    for g in range(blocks // GROUP):
        write(g).wait()


def placed(rows, first, height, width):
    return jnp.pad(rows, ((first, height - first - rows.shape[0]), (0, width - rows.shape[1])))


def local(sizes, labels, weights, column_index, send_index, seed_doc, seed_topic):
    blocks, slots, block, _ = weights.shape
    topics = labels.shape[1]
    dirs, sends = send_index.shape[1:]
    halo = dirs * sends
    chunks = blocks // CHUNK
    seeds = seed_doc.shape[0]
    put = functools.partial(placed, height=24, width=seeds)
    table = put(column_index.T, 0) + put(send_index.reshape(dirs, sends), slots)
    table += put(seed_doc.reshape(1, seeds), 16) + put(seed_topic.reshape(1, seeds), 17)
    late, following, partial, scale = pl.pallas_call(
        functools.partial(spread_kernel, sizes),
        out_shape=(
            jax.ShapeDtypeStruct((blocks, slots - EARLY, block, block), BF16),
            jax.ShapeDtypeStruct((blocks + halo, block, topics), BF16),
            jax.ShapeDtypeStruct((blocks, block, topics), F32),
            jax.ShapeDtypeStruct((blocks, block, block), F32),
        ),
        in_specs=[VMEM, HBM, HBM],
        out_specs=(VMEM, VMEM, VMEM, VMEM),
        scratch_shapes=[
            pltpu.SMEM((16, 128), jnp.int32),
            pltpu.VMEM((blocks, EARLY, block, block), BF16),
            pltpu.VMEM((blocks, block, topics), F32),
            pltpu.VMEM((blocks + halo, block, topics), BF16),
            pltpu.VMEM((dirs, sends, block, topics), F32),
            pltpu.VMEM((FILLED, block, topics), F32),
            pltpu.VMEM((blocks, block, topics), BF16),
            pltpu.VMEM((seed_doc.shape[0], topics), BF16),
            pltpu.VMEM((dirs, sends, block, topics), BF16),
            pltpu.VMEM((dirs, sends, block, topics), BF16),
            pltpu.VMEM((dirs, sends, block, topics), BF16),
            pltpu.VMEM((blocks, block, topics), BF16),
            pltpu.VMEM((dirs, 8, block), F32),
            pltpu.VMEM((dirs, 8, block), F32),
            pltpu.SemaphoreType.DMA,
            pltpu.SemaphoreType.DMA,
            pltpu.SemaphoreType.DMA((chunks,)),
            pltpu.SemaphoreType.DMA((chunks,)),
            pltpu.SemaphoreType.DMA((dirs,)),
            pltpu.SemaphoreType.DMA((dirs,)),
            pltpu.SemaphoreType.DMA((dirs, sends)),
            pltpu.SemaphoreType.DMA((dirs, sends)),
            pltpu.SemaphoreType.DMA((dirs,)),
            pltpu.SemaphoreType.DMA((dirs,)),
        ],
        compiler_params=pltpu.CompilerParams(
            collective_id=0, has_side_effects=True, vmem_limit_bytes=38 << 20
        ),
        name="spread",
    )(
        table,
        labels.reshape(blocks, block, topics),
        weights,
    )
    out = pl.pallas_call(
        finish_kernel,
        out_shape=jax.ShapeDtypeStruct((blocks, block, topics), F32),
        in_specs=[VMEM, VMEM, VMEM, VMEM, VMEM],
        out_specs=HBM,
        scratch_shapes=[
            pltpu.SMEM((16, 128), jnp.int32),
            pltpu.VMEM((blocks, block, topics), F32),
            pltpu.SemaphoreType.DMA,
            pltpu.SemaphoreType.DMA((blocks // GROUP,)),
        ],
        compiler_params=pltpu.CompilerParams(vmem_limit_bytes=30 << 20),
        name="finish",
    )(table, late, following, partial, scale)
    return out.reshape(blocks * block, topics)


def solution(mesh):
    sizes = (mesh.shape["gx"], mesh.shape["gy"])
    parts = P(("gx", "gy"))
    return jax.shard_map(
        functools.partial(local, sizes),
        mesh=mesh,
        in_specs=(parts,) * 6,
        out_specs=parts,
        check_vma=False,
    )
```

```python
import functools

import jax
import jax.numpy as jnp
from jax import lax
from jax.experimental import pallas as pl
from jax.experimental.pallas import tpu as pltpu
from jax.sharding import PartitionSpec as P

ALPHA = 0.99
GAIN = 1.0 / (1.0 - 0.99)
SEED = (1.0 - ALPHA) * GAIN

MESH = pl.DeviceIdType.MESH
BF16 = jnp.bfloat16
F32 = jnp.float32
VMEM = pl.BlockSpec(memory_space=pltpu.VMEM)
SMEM = pl.BlockSpec(memory_space=pltpu.SMEM)
HBM = pl.BlockSpec(memory_space=pl.ANY)

EARLY = 8
CHUNK = 4
FILLED = 16
WIDE = 16
GROUP = 4
DIRS = (2, 3, 0, 1)


def block_row(parts, labels_ref, table_ref, row):
    left, right = [], []
    for weight_ref, first in parts:
        for k in range(weight_ref.shape[1]):
            left.append(weight_ref[row, k])
            right.append(labels_ref[table_ref[first + k, row]])
    return jnp.dot(
        jnp.concatenate(left, axis=1),
        jnp.concatenate(right, axis=0),
        preferred_element_type=F32,
    )


def doubled(scale):
    return jnp.concatenate([scale, scale], axis=1)


def spread_kernel(
    sizes,
    columns_hbm,
    lists_hbm,
    docs_hbm,
    topics_hbm,
    labels_hbm,
    weights_hbm,
    late_ref,
    next_ref,
    partial_ref,
    scale_ref,
    columns_ref,
    table_ref,
    list_ref,
    doc_ref,
    topic_ref,
    early_ref,
    labels_ref,
    now_ref,
    first_ref,
    fill_ref,
    count_ref,
    hot_ref,
    stage_a,
    stage_b,
    halo_a,
    mine_ref,
    rows_out,
    rows_in,
    table_sem,
    label_sem,
    early_sem,
    late_sem,
    send_a,
    recv_a,
    send_b,
    recv_b,
    send_s,
    recv_s,
):
    outer, inner = sizes
    blocks, block, topics = labels_hbm.shape
    seeds = docs_hbm.shape[1]
    sends = halo_a.shape[1]
    a, b = lax.axis_index("gx"), lax.axis_index("gy")
    has = [b > 0, b < inner - 1, a > 0, a < outer - 1]
    peer = [
        {"gx": a, "gy": b - 1},
        {"gx": a, "gy": b + 1},
        {"gx": a - 1, "gy": b},
        {"gx": a + 1, "gy": b},
    ]

    def remote(src, dst, send_sem, recv_sem, d):
        return pltpu.make_async_remote_copy(
            src_ref=src,
            dst_ref=dst,
            send_sem=send_sem,
            recv_sem=recv_sem,
            device_id=peer[d],
            device_id_type=MESH,
        )

    chunks = blocks // CHUNK
    label_copy = pltpu.make_async_copy(labels_hbm, labels_ref, label_sem)

    def early_copy(c):
        rows = pl.ds(c * CHUNK, CHUNK)
        return pltpu.make_async_copy(
            weights_hbm.at[rows, pl.ds(0, EARLY)], early_ref.at[rows], early_sem.at[c]
        )

    def late_copy(c):
        rows = pl.ds(c * CHUNK, CHUNK)
        late = weights_hbm.shape[1] - EARLY
        return pltpu.make_async_copy(
            weights_hbm.at[rows, pl.ds(EARLY, late)], late_ref.at[rows], late_sem.at[c]
        )

    label_copy.start()
    small = [
        pltpu.make_async_copy(lists_hbm, list_ref, table_sem.at[0]),
        pltpu.make_async_copy(columns_hbm, table_ref, table_sem.at[1]),
        pltpu.make_async_copy(docs_hbm, doc_ref, table_sem.at[2]),
        pltpu.make_async_copy(topics_hbm, topic_ref, table_sem.at[3]),
        pltpu.make_async_copy(columns_hbm, columns_ref, table_sem.at[4]),
    ]
    for copy in small:
        copy.start()
    for c in range(chunks):
        early_copy(c).start(priority=1)
        late_copy(c).start(priority=1)

    barrier = pltpu.get_barrier_semaphore()
    for d in range(4):

        @pl.when(has[d])
        def _():
            pl.semaphore_signal(barrier, inc=1, device_id=peer[d], device_id_type=MESH)

    pl.semaphore_wait(barrier, sum(jnp.where(h, 1, 0) for h in has))

    for copy in small:
        copy.wait()
    label_copy.wait()
    for d in DIRS:
        for s in range(sends):
            stage_a[d, s] = labels_ref[list_ref[d, s]].astype(BF16)

        @pl.when(has[d])
        def _():
            remote(stage_a.at[d], halo_a.at[d ^ 1], send_a.at[d], recv_a.at[d ^ 1], d).start()

    wanted = jnp.broadcast_to(topic_ref[...], (topics, seeds))
    ours = lax.broadcasted_iota(jnp.int32, (topics, seeds), 0)
    hot_ref[...] = jnp.where(wanted == ours, 1.0, 0.0).astype(F32).T.astype(BF16)

    wanted_docs = jnp.broadcast_to(doc_ref[...], (block, seeds))

    def count_rows(g, carry):
        for u in range(CHUNK):
            r = g * CHUNK + u
            docs = lax.broadcasted_iota(jnp.int32, (block, seeds), 0) + r * block
            hot = jnp.where(docs == wanted_docs, 1.0, 0.0)
            found = jnp.dot(hot.astype(BF16), hot_ref[...], preferred_element_type=F32)
            count_ref[r] = found.astype(BF16)
        return carry

    lax.fori_loop(0, chunks, count_rows, 0)

    def degree_rows(c, carry):
        early_copy(c).wait()
        late_copy(c).wait()
        for u in range(CHUNK):
            r = c * CHUNK + u
            total = early_ref[r, 0].astype(F32)
            for k in range(1, EARLY):
                total = total + early_ref[r, k].astype(F32)
            for k in range(late_ref.shape[1]):
                total = total + late_ref[r, k].astype(F32)
            degree = jnp.sum(total, axis=1, keepdims=True)
            scale = jnp.broadcast_to(1.0 / jnp.sqrt(degree), (block, block))
            scale_ref[r] = scale
            now_ref[r] = (doubled(scale) * labels_ref[r]).astype(BF16)
        return carry

    lax.fori_loop(0, chunks, degree_rows, 0)

    lanes = lax.broadcasted_iota(jnp.int32, (block, block), 1)
    columns = jnp.zeros((block, block), F32)
    for d in range(4):
        for s in range(sends):
            columns = jnp.where(lanes == d * 8 + s, scale_ref[list_ref[d, s]], columns)
    rows = columns.T
    for d in DIRS:
        rows_out[d] = rows[d * 8 : d * 8 + 8]

        @pl.when(has[d])
        def _():
            remote(rows_out.at[d], rows_in.at[d ^ 1], send_s.at[d], recv_s.at[d ^ 1], d).start()

    def sent_early(g, carry):
        for u in range(2):
            for d in DIRS:
                i = g * 2 + u
                row = list_ref[d, i]
                first_ref[d, i] = block_row([(early_ref, 0)], now_ref, table_ref, row)
        return carry

    lax.fori_loop(0, sends // 2, sent_early, 0)

    def fill_rows(g, carry):
        for u in range(WIDE):
            r = g * WIDE + u
            fill_ref[r] = block_row([(early_ref, 0)], now_ref, table_ref, r)
        return carry

    lax.fori_loop(0, FILLED // WIDE, fill_rows, 0)

    for d in range(4):

        @pl.when(has[d])
        def _():
            remote(rows_out.at[d], rows_in.at[d], send_s.at[d], recv_s.at[d], d).wait_recv()

        @pl.when(jnp.logical_not(has[d]))
        def _():
            rows_in[d] = jnp.zeros(rows_in.shape[1:], F32)

    taken = jnp.concatenate(
        [rows_in[d] for d in range(4)] + [jnp.zeros((block - 32, block), F32)], axis=0
    )
    scales = taken.T
    for d in (0, 1, 2, 3):

        @pl.when(has[d])
        def _():
            remote(stage_a.at[d], halo_a.at[d], send_a.at[d], recv_a.at[d], d).wait_recv()

        @pl.when(jnp.logical_not(has[d]))
        def _():
            halo_a[d] = jnp.zeros(halo_a.shape[1:], BF16)

        for s in range(sends):
            scale = jnp.broadcast_to(scales[:, d * 8 + s : d * 8 + s + 1], (block, topics))
            now_ref[blocks + d * sends + s] = (scale * halo_a[d, s].astype(F32)).astype(BF16)

    def next_scaled(r, product):
        scale = doubled(scale_ref[r])
        current = ALPHA * scale * product + SEED * count_ref[r].astype(F32)
        return (scale * current).astype(BF16)

    def halo_copy(d, s):
        block_at = blocks + (d ^ 1) * sends + s
        return remote(
            stage_b.at[d, s], next_ref.at[block_at], send_b.at[d, s], recv_b.at[d ^ 1, s], d
        )

    def halo_arrival(d, s):
        block_at = blocks + d * sends + s
        return remote(
            stage_b.at[d, s], next_ref.at[block_at], send_b.at[d, s], recv_b.at[d, s], d
        )

    for s in range(sends):
        for d in DIRS:
            row = list_ref[d, s]
            late = block_row([(late_ref, EARLY)], now_ref, table_ref, row)
            stage_b[d, s] = next_scaled(row, first_ref[d, s] + late)
        for d in DIRS:

            @pl.when(has[d])
            def _():
                halo_copy(d, s).start()

    def keep(r, product):
        scaled = next_scaled(r, product)
        mine_ref[r] = scaled
        next_ref[r] = scaled

    def filled_rows(g, carry):
        for u in range(WIDE):
            r = g * WIDE + u
            keep(r, fill_ref[r] + block_row([(late_ref, EARLY)], now_ref, table_ref, r))
        return carry

    lax.fori_loop(0, FILLED // WIDE, filled_rows, 0)

    def first_rows(g, carry):
        for u in range(WIDE):
            r = g * WIDE + u
            parts = [(early_ref, 0), (late_ref, EARLY)]
            keep(r, block_row(parts, now_ref, table_ref, r))
        return carry

    lax.fori_loop(FILLED // WIDE, blocks // WIDE, first_rows, 0)

    def second_early(g, carry):
        for u in range(WIDE):
            r = g * WIDE + u
            product = block_row([(early_ref, 0)], mine_ref, table_ref, r)
            scale = doubled(scale_ref[r])
            partial_ref[r] = ALPHA * scale * product + SEED * count_ref[r].astype(F32)
        return carry

    lax.fori_loop(0, blocks // WIDE, second_early, 0)

    for d in range(4):

        @pl.when(has[d])
        def _():
            for s in range(sends):
                halo_arrival(d, s).wait_recv()

        @pl.when(jnp.logical_not(has[d]))
        def _():
            for s in range(sends):
                next_ref[blocks + d * sends + s] = jnp.zeros((block, topics), BF16)

    for d in range(4):

        @pl.when(has[d])
        def _():
            remote(stage_a.at[d], halo_a.at[d], send_a.at[d], recv_a.at[d], d).wait_send()
            remote(rows_out.at[d], rows_in.at[d], send_s.at[d], recv_s.at[d], d).wait_send()
            for s in range(sends):
                halo_arrival(d, s).wait_send()


def finish_kernel(
    table_ref, late_ref, next_ref, partial_ref, scale_ref, out_hbm, out_ref, sems
):
    blocks = out_ref.shape[0]

    def write(g):
        rows = pl.ds(g * GROUP, GROUP)
        return pltpu.make_async_copy(out_ref.at[rows], out_hbm.at[rows], sems.at[g])

    def finish_rows(t, carry):
        for q in range(WIDE // GROUP):
            g = t * (WIDE // GROUP) + q
            for u in range(GROUP):
                r = g * GROUP + u
                product = block_row([(late_ref, EARLY)], next_ref, table_ref, r)
                out_ref[r] = partial_ref[r] + ALPHA * doubled(scale_ref[r]) * product
            write(g).start()
        return carry

    lax.fori_loop(0, blocks // WIDE, finish_rows, 0)
    for g in range(blocks // GROUP):
        write(g).wait()


def in_place(array):
    return pltpu.with_memory_space_constraint(array, pltpu.HBM)


def local(sizes, labels, weights, column_index, send_index, seed_doc, seed_topic):
    blocks, slots, block, _ = weights.shape
    topics = labels.shape[1]
    dirs, sends = send_index.shape[1:]
    halo = dirs * sends
    chunks = blocks // CHUNK
    seeds = seed_doc.shape[0]
    late, following, partial, scale, columns = pl.pallas_call(
        functools.partial(spread_kernel, sizes),
        out_shape=(
            jax.ShapeDtypeStruct((blocks, slots - EARLY, block, block), BF16),
            jax.ShapeDtypeStruct((blocks + halo, block, topics), BF16),
            jax.ShapeDtypeStruct((blocks, block, topics), F32),
            jax.ShapeDtypeStruct((blocks, block, block), F32),
            jax.ShapeDtypeStruct((slots, blocks), jnp.int32),
        ),
        in_specs=[HBM] * 6,
        out_specs=(VMEM,) * 5,
        scratch_shapes=[
            pltpu.SMEM((slots, blocks), jnp.int32),
            pltpu.SMEM((dirs, sends), jnp.int32),
            pltpu.VMEM((1, seeds), jnp.int32),
            pltpu.VMEM((1, seeds), jnp.int32),
            pltpu.VMEM((blocks, EARLY, block, block), BF16),
            pltpu.VMEM((blocks, block, topics), F32),
            pltpu.VMEM((blocks + halo, block, topics), BF16),
            pltpu.VMEM((dirs, sends, block, topics), F32),
            pltpu.VMEM((FILLED, block, topics), F32),
            pltpu.VMEM((blocks, block, topics), BF16),
            pltpu.VMEM((seed_doc.shape[0], topics), BF16),
            pltpu.VMEM((dirs, sends, block, topics), BF16),
            pltpu.VMEM((dirs, sends, block, topics), BF16),
            pltpu.VMEM((dirs, sends, block, topics), BF16),
            pltpu.VMEM((blocks, block, topics), BF16),
            pltpu.VMEM((dirs, 8, block), F32),
            pltpu.VMEM((dirs, 8, block), F32),
            pltpu.SemaphoreType.DMA((5,)),
            pltpu.SemaphoreType.DMA,
            pltpu.SemaphoreType.DMA((chunks,)),
            pltpu.SemaphoreType.DMA((chunks,)),
            pltpu.SemaphoreType.DMA((dirs,)),
            pltpu.SemaphoreType.DMA((dirs,)),
            pltpu.SemaphoreType.DMA((dirs, sends)),
            pltpu.SemaphoreType.DMA((dirs, sends)),
            pltpu.SemaphoreType.DMA((dirs,)),
            pltpu.SemaphoreType.DMA((dirs,)),
        ],
        compiler_params=pltpu.CompilerParams(
            collective_id=0, has_side_effects=True, vmem_limit_bytes=38 << 20
        ),
        name="spread",
    )(
        in_place(column_index.T),
        in_place(send_index.reshape(dirs, sends)),
        in_place(seed_doc.reshape(1, seeds)),
        in_place(seed_topic.reshape(1, seeds)),
        labels.reshape(blocks, block, topics),
        weights,
    )
    out = pl.pallas_call(
        finish_kernel,
        out_shape=jax.ShapeDtypeStruct((blocks, block, topics), F32),
        in_specs=[SMEM, VMEM, VMEM, VMEM, VMEM],
        out_specs=HBM,
        scratch_shapes=[
            pltpu.VMEM((blocks, block, topics), F32),
            pltpu.SemaphoreType.DMA((blocks // GROUP,)),
        ],
        compiler_params=pltpu.CompilerParams(vmem_limit_bytes=30 << 20),
        name="finish",
    )(columns, late, following, partial, scale)
    return out.reshape(blocks * block, topics)


def solution(mesh):
    sizes = (mesh.shape["gx"], mesh.shape["gy"])
    parts = P(("gx", "gy"))
    return jax.shard_map(
        functools.partial(local, sizes),
        mesh=mesh,
        in_specs=(parts,) * 6,
        out_specs=parts,
        check_vma=False,
    )
```
